128 devices in a mesh: dp: 16 (over y, z_lo, core), tensor: 8 (over z_hi, x).
Axes of the slice: x: 4, y: 4, z: 4 (z_hi: 2, z_lo: 2; z = z_hi * 2 + z_lo), core: 2. Of those that a mesh axis runs over, the one named last changes fastest.
Arguments:
- latents: bfloat16 [16, 16, 1280, 128], P(None, 'dp', 'tensor'), may hold values from -6 to 6
- kernel: bfloat16 [9, 16, 8, 12800], P(None, 'dp', 'tensor'), may hold values from -0.0546875 to 0.0546875
- out_grad: bfloat16 [16, 16, 128, 1280], P('tensor', 'dp'), may hold values from -6 to 6
Outputs:
- conv_out: bfloat16 [16, 16, 128, 1280], P('tensor', 'dp')
- in_grad: bfloat16 [16, 16, 1280, 128], P(None, 'dp', 'tensor')
- kernel_grad: float32 [9, 16, 8, 12800], P(None, 'dp', 'tensor')
The draws below stay inside these ranges and needn't reach their ends.
All inputs are finite; a program needn't handle non-finite values.
Results may differ from the reference program's by a relative error of at most 0.001.
Values may be sent and summed in bfloat16 or wider, within the bound.
A program may use at most 256 MiB of HBM per device.

```python
import jax
import jax.numpy as jnp

C = 1280
W = 128
H = 16
B = 16
N_DP = 16
N_TENSOR = 8


def raised(array, rng, source, target, blocks, factor):
    def block_of(dim):
        return (jnp.arange(array.shape[dim]) // (array.shape[dim] // blocks)).reshape((-1,) + (1,) * (array.ndim - 1 - dim))

    one_side = jax.random.permutation(rng, blocks)[block_of(target)]
    other_side = (block_of(target) + blocks // 2) % blocks
    return jnp.where((block_of(source) == one_side) | (block_of(source) == other_side), factor * array, array)


def steps_of(stream_key, shape, cuts, smallest, high):
    gain = 1.0
    for position, parts in cuts:
        draws = jax.random.uniform(jax.random.fold_in(jax.random.fold_in(stream_key, 6), position), (parts,), jnp.float32, smallest / len(cuts), high / len(cuts))
        gain = gain * jnp.repeat(jnp.exp(draws), shape[position] // parts).reshape((-1,) + (1,) * (len(shape) - 1 - position))
    return gain


def noise(own_key, shape, deviation, reach, shards=(), held_as=jnp.bfloat16):
    values = jax.random.normal(own_key, shape, jnp.float32) * deviation
    if len(shards) > 0:
        values = steps_of(own_key, shape, shards, -0.22, 0.18) * values
    return jnp.clip(values, min=-reach, max=reach).astype(held_as)


def gaussian_with(rng, extent, deviation, most, shards, heavy, held_as=jnp.bfloat16):
    entries = deviation * jax.random.normal(rng, extent, jnp.float32)
    if shards:
        entries = entries * steps_of(rng, extent, shards, -0.22, 0.18)
    return jnp.clip(raised(entries, jax.random.fold_in(rng, 3), *heavy), -most, most).astype(held_as)


def setup_inputs(seed: int = 0) -> dict:
    keys = jax.random.split(jax.random.key(seed), 4)
    latents = gaussian_with(keys[0], (H, B, C, W), 1.0, 6.0, ((1, 16), (2, 8)), (2, 0, 8, 2.0))
    kernel = noise(keys[1], (9, N_DP, N_TENSOR, (C // N_DP) * (C // N_TENSOR)), (9 * C) ** -0.5, 0.0546875, ((1, 16), (2, 8)))
    out_grad = gaussian_with(keys[2], (H, B, W, C), 1.0, 6.0, ((0, 8), (1, 16)), (1, 3, 16, 2.0))
    return {"latents": latents, "kernel": kernel, "out_grad": out_grad}


def reference(latents, kernel, out_grad):
    col_out = C // N_DP
    col_in = C // N_TENSOR
    rows_all = latents.shape[0]
    cols_all = latents.shape[3]
    kernel_f = kernel.astype(jnp.float32).reshape(9, N_DP, N_TENSOR, col_out, col_in)
    kernel_f = kernel_f.transpose(1, 3, 0, 2, 4).reshape(C, 9, C)
    lat = latents.transpose(0, 1, 3, 2)
    padded = jnp.pad(lat, ((1, 1), (0, 0), (1, 1), (0, 0))).astype(jnp.float32)
    grad_f = out_grad.astype(jnp.float32)
    grad_padded = jnp.pad(grad_f, ((1, 1), (0, 0), (1, 1), (0, 0)))
    conv_sum = jnp.zeros(out_grad.shape, jnp.float32)
    back_sum = jnp.zeros(lat.shape, jnp.float32)
    grads = []
    for row_tap in range(3):
        for col_tap in range(3):
            tap = 3 * row_tap + col_tap
            window = padded[row_tap:row_tap + rows_all, :, col_tap:col_tap + cols_all, :]
            conv_sum = conv_sum + jnp.einsum('hbwi,oi->hbwo', window, kernel_f[:, tap, :])
            shifted = grad_padded[2 - row_tap:2 - row_tap + rows_all, :, 2 - col_tap:2 - col_tap + cols_all, :]
            back_sum = back_sum + jnp.einsum('hbwo,oi->hbwi', shifted, kernel_f[:, tap, :])
            grads.append(jnp.einsum('hbwo,hbwi->oi', grad_f, window))
    kernel_grad = jnp.stack(grads, axis=1)
    kernel_grad = kernel_grad.reshape(N_DP, col_out, 9, N_TENSOR, col_in).transpose(2, 0, 3, 1, 4)
    kernel_grad = kernel_grad.reshape(9, N_DP, N_TENSOR, col_out * col_in)
    in_grad = back_sum.astype(jnp.bfloat16).transpose(0, 1, 3, 2)
    return conv_sum.astype(jnp.bfloat16), in_grad, kernel_grad
```

```python
import jax
import jax.numpy as jnp
from jax import lax
from jax.experimental import pallas as pl
from jax.experimental.pallas import tpu as pltpu
from jax.sharding import PartitionSpec as P

BF = jnp.bfloat16
F32 = jnp.float32
N_COPIES = 36


def dot_nt(a, b):
    return lax.dot_general(a, b, (((1,), (1,)), ((), ())), preferred_element_type=F32)


def three_shifts(row):
    wide = row.astype(F32)
    lane = lax.broadcasted_iota(jnp.int32, wide.shape, 1)
    first = jnp.where(lane == 0, 0.0, pltpu.roll(wide, 1, 1))
    last = jnp.where(lane == 127, 0.0, pltpu.roll(wide, 127, 1))
    zeros = jnp.zeros((32, 128), F32)
    return jnp.concatenate([first, wide, last, zeros], axis=0)


def body(
    g_ref, x_ref, k_ref,
    conv_ref, in_ref, kgrad_ref,
    g_pad, gt, kall, xz, xv, xt, f, xa, xb, xl, xr, p, r1, ya, yb, yl, yr, zr,
    ss, rs,
):
    t = lax.axis_index("tensor")
    d = lax.axis_index("dp")
    zh, x = t // 4, t % 4
    y, zl, c = d // 4, (d // 2) % 2, d % 2
    e = d // 2
    x_right, x_left, x_far = (x + 1) % 4, (x + 3) % 4, (x + 2) % 4
    y_right, y_left, y_far = (y + 1) % 4, (y + 3) % 4, (y + 2) % 4
    oz = 1 - zh
    e_other = y * 2 + 1 - zl

    to_z = {"tensor": oz * 4 + x}
    to_xr = {"tensor": zh * 4 + x_right}
    to_xl = {"tensor": zh * 4 + x_left}
    to_yr = {"dp": y_right * 4 + zl * 2 + c}
    to_yl = {"dp": y_left * 4 + zl * 2 + c}
    to_zl = {"dp": y * 4 + (1 - zl) * 2 + c}
    to_core = {"dp": y * 4 + zl * 2 + 1 - c}

    barrier = pltpu.get_barrier_semaphore()
    for peer in (to_z, to_xr, to_xl, to_yr, to_yl, to_zl, to_core):
        pl.semaphore_signal(barrier, inc=1, device_id=peer, device_id_type=pl.DeviceIdType.MESH)
    pl.semaphore_wait(barrier, 7)

    def copy(n, s=None):
        src, dst, peer = plan[n]() if s is None else plan[n](s)
        at = n if s is None else n + s
        return pltpu.make_async_remote_copy(
            src_ref=src,
            dst_ref=dst,
            send_sem=ss.at[at],
            recv_sem=rs.at[at],
            device_id=peer,
            device_id_type=pl.DeviceIdType.MESH,
        )

    def start(*numbers):
        for n in numbers:
            copy(n).start()

    def got(*numbers):
        for n in numbers:
            copy(n).wait_recv()

    def rows_of(z_part, x_part):
        return g_pad.at[pl.ds(1 + 2 * (z_part * 4 + x_part), 2)]

    def row_of(z_part, x_part, which):
        return g_pad.at[pl.ds(1 + 2 * (z_part * 4 + x_part) + which, 1)]

    def same(ref, peer):
        return ref, ref, peer

    def mine():
        return rows_of(zh, x)

    def pair(block):
        return kall.at[block, c]

    def pairs(y_part):
        return kall.at[pl.ds(2 * y_part, 2), c]

    def yq_of(s):
        return (y + 2 + 3 * s) % 4

    plan = {
        0: lambda: (g_ref, mine(), to_z),
        1: lambda: (g_ref, mine(), to_xr),
        2: lambda: (g_ref, mine(), to_xl),
        3: lambda: same(rows_of(oz, x), to_xr),
        4: lambda: same(rows_of(oz, x), to_xl),
        5: lambda: same(row_of(zh, x_left, 0), to_xr),
        6: lambda: same(row_of(zh, x_right, 1), to_xl),
        7: lambda: same(row_of(oz, x_left, 0), to_xr),
        8: lambda: same(row_of(oz, x_right, 1), to_xl),
        9: lambda: (x_ref.at[pl.ds(7 * oz, 9)], xz, to_z),
        10: lambda: (k_ref, kall.at[e, c, 1], to_z),
        11: lambda: same(pair(e), to_zl),
        13: lambda: same(pair(e), to_yr),
        14: lambda: same(pair(e), to_yl),
        15: lambda: same(pair(e_other), to_yr),
        16: lambda: same(pair(e_other), to_yl),
        17: lambda: same(pair(y_left * 2 + zl), to_yr),
        18: lambda: same(pair(y_right * 2 + 1 - zl), to_yl),
        19: lambda: same(pairs(y), to_core),
        20: lambda: same(pairs(y_left), to_core),
        21: lambda: same(pairs(y_right), to_core),
        22: lambda: same(pairs(y_far), to_core),
        23: lambda: (f.at[x_far, 0], xa, to_xr),
        24: lambda: (f.at[x_far, 1], xb, to_xl),
        25: lambda: (f.at[x_right], xl, to_xr),
        26: lambda: (f.at[x_left], xr, to_xl),
        27: lambda s: (
            p.at[pl.ds(2 * yq_of(s), 2), 1 - c],
            r1.at[pl.ds(2 * yq_of(s), 2)],
            to_core,
        ),
        31: lambda: (r1.at[2 * y_far], ya, to_yr),
        32: lambda: (r1.at[2 * y_far + 1], yb, to_yl),
        33: lambda: (r1.at[pl.ds(2 * y_right, 2)], yl, to_yr),
        34: lambda: (r1.at[pl.ds(2 * y_left, 2)], yr, to_yl),
        35: lambda: (r1.at[2 * y + 1 - zl], zr, to_zl),
    }

    start(10, 0, 1, 2, 9)

    kall[e, c, 0] = k_ref[...]
    g_pad[pl.ds(1 + 2 * t, 2)] = g_ref[...]
    g_pad[0] = jnp.zeros((128, 1280), BF)
    g_pad[17] = jnp.zeros((128, 1280), BF)

    def turn(z_part, x_part):
        at = z_part * 4 + x_part
        block = g_pad[pl.ds(1 + 2 * at, 2)].reshape(256, 1280)
        gt[:, :, pl.ds(pl.multiple_of(at * 256, 256), 256)] = block.T.reshape(16, 80, 256)

    got(10)
    start(11)
    start(13)
    start(14)

    xv[:, 0:128] = jnp.zeros((512, 128), BF)
    xv[:, 17 * 128 : 18 * 128] = jnp.zeros((512, 128), BF)

    def own_row(k, _):
        at = pl.multiple_of((k + 1) * 128, 128)
        xv[:, pl.ds(at, 128)] = three_shifts(x_ref[k]).astype(BF)
        return 0

    lax.fori_loop(0, 16, own_row, 0)

    got(11)
    start(15)
    start(16)
    start(19)

    xt[0, 9 * zh] = jnp.zeros((128, 512), BF)
    xt[1, 9 * zh] = jnp.zeros((128, 512), BF)

    def own_turned(k, _):
        xt[0, k + 1 - zh] = three_shifts(x_ref[7 * zh + k]).T.astype(BF)
        return 0

    lax.fori_loop(0, 9, own_turned, 0)

    turn(zh, x)
    got(0)
    start(3)
    start(4)
    turn(oz, x)
    got(1, 2)
    start(5)
    start(6)

    got(13, 16)
    start(17)
    start(18)
    got(15)
    start(20)
    got(14)
    start(21)

    turn(zh, x_left)
    turn(zh, x_right)
    got(9)

    def other_turned(k, _):
        xt[1, k + 1 - zh] = three_shifts(xz[k]).T.astype(BF)
        return 0

    lax.fori_loop(0, 9, other_turned, 0)

    got(3, 4)
    start(7)
    start(8)
    got(17, 18)
    start(22)
    turn(oz, x_left)
    turn(oz, x_right)
    got(19, 20, 21, 22)

    def forward(s, _):
        xq = (x + 2 + 3 * s) % 4
        left = jnp.concatenate(
            [xt[j, pl.ds(2 * xq + u, 2)].reshape(256, 512) for j in range(2) for u in range(3)],
            axis=1,
        )
        right = jnp.concatenate(
            [kall[:, :, j, u].reshape(1280, 512) for j in range(2) for u in range(3)], axis=1
        )
        f[xq] = dot_nt(left, right).reshape(2, 128, 1280)

        @pl.when(s == 0)
        def _():
            start(23)
            start(24)

        return 0

    lax.fori_loop(0, 4, forward, 0)

    got(5, 6, 7, 8)
    turn(zh, x_far)
    turn(oz, x_far)

    def kernel_terms(s, _):
        yq = yq_of(s)
        left = gt[pl.ds(4 * yq, 4)].reshape(320, 2048)
        for u in range(3):
            part = dot_nt(left, xv[:, u * 128 : u * 128 + 2048])
            p[pl.ds(2 * yq, 2), :, u] = part.reshape(2, 2, 80, 512)
        copy(27, s).start()

        @pl.when(s == 1)
        def _():
            got(23)
            f[x_right, 0] = f[x_right, 0] + xa[...]
            start(25)
            got(24)
            f[x_left, 1] = f[x_left, 1] + xb[...]
            start(26)

        @pl.when(s == 2)
        def _():
            joined(0)
            start(31)
            start(32)

        return 0

    def joined(s):
        yq = yq_of(s)
        copy(27, s).wait_recv()
        for k in range(2):
            r1[2 * yq + k] = r1[2 * yq + k] + p[2 * yq + k, c]

    lax.fori_loop(0, 4, kernel_terms, 0)

    lane = lax.broadcasted_iota(jnp.int32, (160, 128), 1)

    def input_grad(s, _):
        left = jnp.concatenate(
            [g_pad[pl.ds(4 * s + 2 - u, 4)].reshape(512, 1280) for u in range(3)], axis=1
        )
        right = jnp.concatenate([kall[:, :, 0, u].reshape(1280, 512) for u in range(3)], axis=0)
        turned = jnp.dot(left, right, preferred_element_type=F32).T
        for k in range(4):
            at = slice(k * 128, (k + 1) * 128)
            first = jnp.where(lane == 127, 0.0, pltpu.roll(turned[0:160, at], 127, 1))
            last = jnp.where(lane == 0, 0.0, pltpu.roll(turned[320:480, at], 1, 1))
            in_ref[4 * s + k] = (first + turned[160:320, at] + last).astype(BF)

        @pl.when(s == 0)
        def _():
            joined(1)
            joined(3)

        @pl.when(s == 1)
        def _():
            got(31)
            r1[2 * y_right] = r1[2 * y_right] + ya[...]
            start(33)
            got(32)
            r1[2 * y_left + 1] = r1[2 * y_left + 1] + yb[...]
            start(34)

        return 0

    lax.fori_loop(0, 4, input_grad, 0)

    joined(2)
    got(25, 26)
    for k in range(2):
        conv_ref[k] = (f[x, k] + xl[k] + xr[k]).astype(BF)
    got(33, 34)
    for k in range(2):
        r1[2 * y + k] = r1[2 * y + k] + yl[k] + yr[k]
    start(35)
    got(35)
    kgrad_ref[...] = r1[2 * y + zl] + zr[...]

    for n in plan:
        if n != 27:
            copy(n).wait_send()
    for s in range(4):
        copy(27, s).wait_send()


def on_device(latents, kernel, out_grad):
    g = out_grad.reshape(2, 128, 1280)
    xs = latents.reshape(16, 160, 128)
    k = kernel.reshape(3, 3, 80, 160).transpose(0, 2, 1, 3).reshape(3, 80, 480)
    k = jnp.pad(k, ((0, 0), (0, 0), (0, 32)))
    vmem = pl.BlockSpec(memory_space=pltpu.VMEM)
    scratch = [
        ((18, 128, 1280), BF),
        ((16, 80, 2048), BF),
        ((8, 2, 2, 3, 80, 512), BF),
        ((9, 160, 128), BF),
        ((512, 2304), BF),
        ((2, 10, 128, 512), BF),
        ((4, 2, 128, 1280), F32),
        ((128, 1280), F32),
        ((128, 1280), F32),
        ((2, 128, 1280), F32),
        ((2, 128, 1280), F32),
        ((8, 2, 3, 80, 512), F32),
        ((8, 3, 80, 512), F32),
        ((3, 80, 512), F32),
        ((3, 80, 512), F32),
        ((2, 3, 80, 512), F32),
        ((2, 3, 80, 512), F32),
        ((3, 80, 512), F32),
    ]
    conv, grad, kgrad = pl.pallas_call(
        body,
        out_shape=(
            jax.ShapeDtypeStruct((2, 128, 1280), BF),
            jax.ShapeDtypeStruct((16, 160, 128), BF),
            jax.ShapeDtypeStruct((3, 80, 512), F32),
        ),
        in_specs=[vmem] * 3,
        out_specs=(vmem, vmem, vmem),
        scratch_shapes=[pltpu.VMEM(shape, dtype) for shape, dtype in scratch]
        + [pltpu.SemaphoreType.DMA((N_COPIES,)), pltpu.SemaphoreType.DMA((N_COPIES,))],
        compiler_params=pltpu.CompilerParams(
            collective_id=0, has_side_effects=True, vmem_limit_bytes=67043328
        ),
        name="conv_all",
    )(g, xs, k)
    kgrad = kgrad[:, :, :480].reshape(3, 80, 3, 160).transpose(0, 2, 1, 3)
    return (
        conv.reshape(2, 1, 128, 1280),
        grad.reshape(16, 1, 160, 128),
        kgrad.reshape(9, 1, 1, 12800),
    )


def solution(mesh):
    return jax.shard_map(
        on_device,
        mesh=mesh,
        in_specs=(
            P(None, "dp", "tensor", None),
            P(None, "dp", "tensor", None),
            P("tensor", "dp", None, None),
        ),
        out_specs=(
            P("tensor", "dp", None, None),
            P(None, "dp", "tensor", None),
            P(None, "dp", "tensor", None),
        ),
        check_vma=False,
    )
```

```python
import jax
import jax.numpy as jnp
from jax import lax
from jax.experimental import pallas as pl
from jax.experimental.pallas import tpu as pltpu
from jax.sharding import PartitionSpec as P

BF = jnp.bfloat16
F32 = jnp.float32
N_COPIES = 49


def dot_nt(a, b):
    return lax.dot_general(a, b, (((1,), (1,)), ((), ())), preferred_element_type=F32)


def three_shifts(row):
    wide = row.astype(F32)
    lane = lax.broadcasted_iota(jnp.int32, wide.shape, 1)
    first = jnp.where(lane == 0, 0.0, pltpu.roll(wide, 1, 1))
    last = jnp.where(lane == 127, 0.0, pltpu.roll(wide, 127, 1))
    zeros = jnp.zeros((32, 128), F32)
    return jnp.concatenate([first, wide, last, zeros], axis=0)


def body(
    g_ref, x_ref, k_ref,
    conv_ref, in_ref, kgrad_ref,
    g_pad, gt, kall, xz, xv, xt, f, xa, xb, xl, xr, p, r1, ya, yb, yl, yr, zr,
    ss, rs, sc,
):
    t = lax.axis_index("tensor")
    d = lax.axis_index("dp")
    zh, x = t // 4, t % 4
    y, zl, c = d // 4, (d // 2) % 2, d % 2
    e = d // 2
    x_right, x_left, x_far = (x + 1) % 4, (x + 3) % 4, (x + 2) % 4
    y_right, y_left, y_far = (y + 1) % 4, (y + 3) % 4, (y + 2) % 4
    oz = 1 - zh
    e_other = y * 2 + 1 - zl

    to_z = {"tensor": oz * 4 + x}
    to_xr = {"tensor": zh * 4 + x_right}
    to_xl = {"tensor": zh * 4 + x_left}
    to_yr = {"dp": y_right * 4 + zl * 2 + c}
    to_yl = {"dp": y_left * 4 + zl * 2 + c}
    to_zl = {"dp": y * 4 + (1 - zl) * 2 + c}
    to_core = {"dp": y * 4 + zl * 2 + 1 - c}
    to_zx = {"tensor": oz * 4 + x, "dp": y * 4 + (1 - zl) * 2 + c}

    barrier = pltpu.get_barrier_semaphore()
    for peer in (to_z, to_xr, to_xl, to_yr, to_yl, to_zl, to_zx, to_core):
        pl.semaphore_signal(barrier, inc=1, device_id=peer, device_id_type=pl.DeviceIdType.MESH)
    pl.semaphore_wait(barrier, 8)

    def copy(n):
        src, dst, peer = plan[n]()
        return pltpu.make_async_remote_copy(
            src_ref=src,
            dst_ref=dst,
            send_sem=ss.at[n],
            recv_sem=rs.at[n],
            device_id=peer,
            device_id_type=pl.DeviceIdType.MESH,
        )

    def start(*numbers):
        for n in numbers:
            copy(n).start()

    def got(*numbers):
        for n in numbers:
            copy(n).wait_recv()

    def row_of(z_part, x_part, which):
        return g_pad.at[1 + 2 * (z_part * 4 + x_part) + which]

    def same(ref, peer):
        return ref, ref, peer

    def pair(block):
        return kall.at[block, c]

    def pairs(y_part):
        return kall.at[pl.ds(2 * y_part, 2), c]

    def part_of(s):
        return (y + 2 + 3 * s) % 4

    def half(ref, which):
        return ref.at[:, which * 40 : which * 40 + 40]

    def first_hop(k, which):
        block = 1 - zl if k == 0 else zl
        return half(r1.at[2 * y_far + block], which), (ya, yb)[which].at[k], (to_yr, to_yl)[which]

    def second_hop(k, way, which):
        block = 1 - zl if k == 0 else zl
        y_part = (y_right, y_left)[way]
        return (
            half(r1.at[2 * y_part + block], which),
            half((yl, yr)[way].at[k], which),
            (to_yr, to_yl)[way],
        )

    plan = {
        0: lambda: (g_ref.at[0], row_of(zh, x, 0), to_z),
        1: lambda: (g_ref.at[1], row_of(zh, x, 1), to_z),
        2: lambda: (k_ref, kall.at[e, c, 1], to_z),
        3: lambda: (k_ref, kall.at[e, c, 0], to_zl),
        4: lambda: (k_ref, kall.at[e, c, 1], to_zx),
        5: lambda: (x_ref.at[pl.ds(7 * oz, 9)], xz, to_z),
        6: lambda: (g_ref.at[0], row_of(zh, x, 0), to_xr),
        7: lambda: (g_ref.at[1], row_of(zh, x, 1), to_xr),
        8: lambda: (g_ref.at[1], row_of(zh, x, 1), to_xl),
        9: lambda: (g_ref.at[0], row_of(zh, x, 0), to_xl),
        10: lambda: same(row_of(zh, x_left, 0), to_xr),
        11: lambda: same(row_of(zh, x_right, 1), to_xl),
        12: lambda: same(row_of(oz, x, 0), to_xr),
        13: lambda: same(row_of(oz, x, 1), to_xr),
        14: lambda: same(row_of(oz, x, 0), to_xl),
        15: lambda: same(row_of(oz, x, 1), to_xl),
        16: lambda: same(row_of(oz, x_left, 0), to_xr),
        17: lambda: same(row_of(oz, x_right, 1), to_xl),
        18: lambda: (k_ref, kall.at[e, c, 0], to_yr),
        19: lambda: (k_ref, kall.at[e, c, 0], to_yl),
        20: lambda: same(kall.at[e, c, 1], to_yr),
        21: lambda: same(kall.at[e, c, 1], to_yl),
        22: lambda: same(pair(e_other), to_yr),
        23: lambda: same(pair(e_other), to_yl),
        24: lambda: same(pair(y_left * 2 + zl), to_yr),
        25: lambda: same(pair(y_right * 2 + 1 - zl), to_yl),
        26: lambda: same(pairs(y), to_core),
        27: lambda: same(pairs(y_left), to_core),
        28: lambda: same(pairs(y_right), to_core),
        29: lambda: same(pairs(y_far), to_core),
        30: lambda: (f.at[x_far, 0], xa, to_xr),
        31: lambda: (f.at[x_far, 1], xb, to_xl),
        32: lambda: (f.at[x_right, 1], xl.at[1], to_xr),
        33: lambda: (f.at[x_left, 0], xr.at[0], to_xl),
        34: lambda: (f.at[x_right, 0], xl.at[0], to_xr),
        35: lambda: (f.at[x_left, 1], xr.at[1], to_xl),
        36: lambda: first_hop(0, 0),
        37: lambda: first_hop(0, 1),
        38: lambda: first_hop(1, 0),
        39: lambda: first_hop(1, 1),
        40: lambda: second_hop(0, 0, 1),
        41: lambda: second_hop(0, 1, 0),
        42: lambda: second_hop(0, 0, 0),
        43: lambda: second_hop(0, 1, 1),
        44: lambda: second_hop(1, 0, 1),
        45: lambda: second_hop(1, 1, 0),
        46: lambda: second_hop(1, 0, 0),
        47: lambda: second_hop(1, 1, 1),
        48: lambda: (r1.at[2 * y + 1 - zl], zr, to_zl),
    }

    def siblings(s):
        return pltpu.make_async_remote_copy(
            src_ref=p.at[pl.ds(2 * part_of(s), 2), 1 - c],
            dst_ref=r1.at[pl.ds(2 * part_of(s), 2)],
            send_sem=sc.at[0, s],
            recv_sem=sc.at[1, s],
            device_id=to_core,
            device_id_type=pl.DeviceIdType.MESH,
        )

    start(2, 6, 8, 18, 19, 3, 4, 7, 9, 0, 1, 5)

    kall[e, c, 0] = k_ref[...]
    g_pad[pl.ds(1 + 2 * t, 2)] = g_ref[...]
    g_pad[0] = jnp.zeros((128, 1280), BF)
    g_pad[17] = jnp.zeros((128, 1280), BF)

    def turn(z_part, x_part):
        at = z_part * 4 + x_part
        block = g_pad[pl.ds(1 + 2 * at, 2)].reshape(256, 1280)
        gt[:, :, pl.ds(pl.multiple_of(at * 256, 256), 256)] = block.T.reshape(16, 80, 256)

    xv[:, 0:128] = jnp.zeros((512, 128), BF)
    xv[:, 17 * 128 : 18 * 128] = jnp.zeros((512, 128), BF)

    def own_row(k, _):
        at = pl.multiple_of((k + 1) * 128, 128)
        xv[:, pl.ds(at, 128)] = three_shifts(x_ref[k]).astype(BF)
        return 0

    lax.fori_loop(0, 16, own_row, 0)

    got(6)
    start(10)
    got(8)
    start(11)

    xt[0, 9 * zh] = jnp.zeros((128, 512), BF)
    xt[1, 9 * zh] = jnp.zeros((128, 512), BF)

    def own_turned(k, _):
        xt[0, k + 1 - zh] = three_shifts(x_ref[7 * zh + k]).T.astype(BF)
        return 0

    lax.fori_loop(0, 9, own_turned, 0)

    got(2)
    start(20, 21)
    got(3, 4)
    start(22, 23, 26)
    turn(zh, x)
    got(18, 20)
    start(24)
    got(0)
    start(12, 14)
    got(7, 9)
    turn(zh, x_left)
    turn(zh, x_right)
    got(1)
    start(13, 15)
    turn(oz, x)
    got(23)
    start(25)
    got(22)
    start(27)
    got(19, 21)
    start(28)
    got(12)
    start(16)
    got(5)

    def other_turned(k, _):
        xt[1, k + 1 - zh] = three_shifts(xz[k]).T.astype(BF)
        return 0

    lax.fori_loop(0, 9, other_turned, 0)

    got(15)
    start(17)
    got(13, 14)
    turn(oz, x_left)
    turn(oz, x_right)
    got(10, 11)
    turn(zh, x_far)
    got(24, 25)
    start(29)
    got(26, 27, 28, 29)

    def forward(xq):
        left = jnp.concatenate(
            [xt[j, pl.ds(2 * xq + u, 2)].reshape(256, 512) for j in range(2) for u in range(3)],
            axis=1,
        )
        right = jnp.concatenate(
            [kall[:, :, j, u].reshape(1280, 512) for j in range(2) for u in range(3)], axis=1
        )
        f[xq] = dot_nt(left, right).reshape(2, 128, 1280)

    def kernel_terms(s, _):
        yq = part_of(s)
        left = gt[pl.ds(4 * yq, 4)].reshape(320, 2048)
        for u in range(3):
            part = dot_nt(left, xv[:, u * 128 : u * 128 + 2048])
            p[pl.ds(2 * yq, 2), :, u] = part.reshape(2, 2, 80, 512)
        siblings(s).start()
        return 0

    def joined(s):
        siblings(s).wait_recv()
        for k in range(2):
            at = 2 * part_of(s) + k
            r1[at] = r1[at] + p[at, c]

    def add_half(k, way):
        block = 1 - zl if k == 0 else zl
        at = 2 * (y_right, y_left)[way] + block
        rows = slice(way * 40, way * 40 + 40)
        r1[at, :, rows] = r1[at, :, rows] + (ya, yb)[way][k]

    forward(x_far)
    start(30, 31)
    got(16, 17)
    turn(oz, x_far)
    lax.fori_loop(0, 2, kernel_terms, 0)
    joined(0)
    start(36, 37, 38, 39)

    def near(s, _):
        forward((x + 1 + 2 * s) % 4)

        @pl.when(s == 0)
        def _():
            start(32)

        return 0

    lax.fori_loop(0, 2, near, 0)
    start(33)
    got(30)
    f[x_right, 0] = f[x_right, 0] + xa[...]
    start(34)
    got(31)
    f[x_left, 1] = f[x_left, 1] + xb[...]
    start(35)

    def last_terms(s, _):
        kernel_terms(5 - s, 0)

        @pl.when(s == 2)
        def _():
            joined(1)
            start(40)

        return 0

    lax.fori_loop(2, 4, last_terms, 0)
    joined(3)
    start(41)
    got(36)
    add_half(0, 0)
    start(42)
    got(37)
    add_half(0, 1)
    start(43, 44, 45)
    got(38)
    add_half(1, 0)
    start(46)
    got(39)
    add_half(1, 1)
    start(47)
    joined(2)
    forward(x)

    lane = lax.broadcasted_iota(jnp.int32, (160, 128), 1)

    def input_grad(s, _):
        left = jnp.concatenate(
            [g_pad[pl.ds(4 * s + 2 - u, 4)].reshape(512, 1280) for u in range(3)], axis=1
        )
        right = jnp.concatenate([kall[:, :, 0, u].reshape(1280, 512) for u in range(3)], axis=0)
        turned = jnp.dot(left, right, preferred_element_type=F32).T
        for k in range(4):
            at = slice(k * 128, (k + 1) * 128)
            first = jnp.where(lane == 127, 0.0, pltpu.roll(turned[0:160, at], 127, 1))
            last = jnp.where(lane == 0, 0.0, pltpu.roll(turned[320:480, at], 1, 1))
            in_ref[4 * s + k] = (first + turned[160:320, at] + last).astype(BF)

        @pl.when(s == 2)
        def _():
            got(40, 41, 42, 43)
            at = 2 * y + 1 - zl
            r1[at] = r1[at] + yl[0] + yr[0]
            start(48)

        return 0

    lax.fori_loop(0, 4, input_grad, 0)

    for k, numbers in ((1, (32, 35)), (0, (33, 34))):
        got(*numbers)
        conv_ref[k] = (f[x, k] + xl[k] + xr[k]).astype(BF)
    got(44, 45, 46, 47)
    r1[2 * y + zl] = r1[2 * y + zl] + yl[1] + yr[1]
    got(48)
    kgrad_ref[...] = r1[2 * y + zl] + zr[...]

    for n in plan:
        copy(n).wait_send()
    for s in range(4):
        siblings(s).wait_send()


def on_device(latents, kernel, out_grad):
    g = out_grad.reshape(2, 128, 1280)
    xs = latents.reshape(16, 160, 128)
    k = kernel.reshape(3, 3, 80, 160).transpose(0, 2, 1, 3).reshape(3, 80, 480)
    k = jnp.pad(k, ((0, 0), (0, 0), (0, 32)))
    vmem = pl.BlockSpec(memory_space=pltpu.VMEM)
    scratch = [
        ((18, 128, 1280), BF),
        ((16, 80, 2048), BF),
        ((8, 2, 2, 3, 80, 512), BF),
        ((9, 160, 128), BF),
        ((512, 2304), BF),
        ((2, 10, 128, 512), BF),
        ((4, 2, 128, 1280), F32),
        ((128, 1280), F32),
        ((128, 1280), F32),
        ((2, 128, 1280), F32),
        ((2, 128, 1280), F32),
        ((8, 2, 3, 80, 512), F32),
        ((8, 3, 80, 512), F32),
        ((2, 3, 40, 512), F32),
        ((2, 3, 40, 512), F32),
        ((2, 3, 80, 512), F32),
        ((2, 3, 80, 512), F32),
        ((3, 80, 512), F32),
    ]
    conv, grad, kgrad = pl.pallas_call(
        body,
        out_shape=(
            jax.ShapeDtypeStruct((2, 128, 1280), BF),
            jax.ShapeDtypeStruct((16, 160, 128), BF),
            jax.ShapeDtypeStruct((3, 80, 512), F32),
        ),
        in_specs=[vmem] * 3,
        out_specs=(vmem, vmem, vmem),
        scratch_shapes=[pltpu.VMEM(shape, dtype) for shape, dtype in scratch]
        + [pltpu.SemaphoreType.DMA(shape) for shape in ((N_COPIES,), (N_COPIES,), (2, 4))],
        compiler_params=pltpu.CompilerParams(
            collective_id=0, has_side_effects=True, vmem_limit_bytes=67043328
        ),
        name="conv_all",
    )(g, xs, k)
    kgrad = kgrad[:, :, :480].reshape(3, 80, 3, 160).transpose(0, 2, 1, 3)
    return (
        conv.reshape(2, 1, 128, 1280),
        grad.reshape(16, 1, 160, 128),
        kgrad.reshape(9, 1, 1, 12800),
    )


def solution(mesh):
    return jax.shard_map(
        on_device,
        mesh=mesh,
        in_specs=(
            P(None, "dp", "tensor", None),
            P(None, "dp", "tensor", None),
            P("tensor", "dp", None, None),
        ),
        out_specs=(
            P("tensor", "dp", None, None),
            P(None, "dp", "tensor", None),
            P(None, "dp", "tensor", None),
        ),
        check_vma=False,
    )
```

```python
import jax
import jax.numpy as jnp
from jax import lax
from jax.experimental import pallas as pl
from jax.experimental.pallas import tpu as pltpu
from jax.sharding import PartitionSpec as P

BF = jnp.bfloat16
F32 = jnp.float32
N_COPIES = 63


def dot_nt(a, b):
    return lax.dot_general(a, b, (((1,), (1,)), ((), ())), preferred_element_type=F32)


def three_shifts(row):
    wide = row.astype(F32)
    lane = lax.broadcasted_iota(jnp.int32, wide.shape, 1)
    first = jnp.where(lane == 0, 0.0, pltpu.roll(wide, 1, 1))
    last = jnp.where(lane == 127, 0.0, pltpu.roll(wide, 127, 1))
    zeros = jnp.zeros((32, 128), F32)
    return jnp.concatenate([first, wide, last, zeros], axis=0)


def body(
    g_ref, x_hbm, k_ref,
    conv_hbm, in_hbm, kgrad_ref,
    x_ref, conv_ref, in_ref,
    g_pad, gt, kall, xz, xv, xt, f, xa, xb, xl, xr, p, r1, ya, yb, yl, yr, zr,
    zb, ba, bb, bl, br, lin,
    ss, rs, sc, lc,
):
    t = lax.axis_index("tensor")
    d = lax.axis_index("dp")
    zh, x = t // 4, t % 4
    y, zl, c = d // 4, (d // 2) % 2, d % 2
    e = d // 2
    x_right, x_left, x_far = (x + 1) % 4, (x + 3) % 4, (x + 2) % 4
    y_right, y_left, y_far = (y + 1) % 4, (y + 3) % 4, (y + 2) % 4
    oz = 1 - zh
    near_half = y // 2
    e_other = y * 2 + 1 - zl

    to_z = {"tensor": oz * 4 + x}
    to_xr = {"tensor": zh * 4 + x_right}
    to_xl = {"tensor": zh * 4 + x_left}
    to_yr = {"dp": y_right * 4 + zl * 2 + c}
    to_yl = {"dp": y_left * 4 + zl * 2 + c}
    to_zl = {"dp": y * 4 + (1 - zl) * 2 + c}
    to_core = {"dp": y * 4 + zl * 2 + 1 - c}
    to_zx = {"tensor": oz * 4 + x, "dp": y * 4 + (1 - zl) * 2 + c}

    barrier = pltpu.get_barrier_semaphore()
    for peer in (to_z, to_xr, to_xl, to_yr, to_yl, to_zl, to_zx, to_core):
        pl.semaphore_signal(barrier, inc=1, device_id=peer, device_id_type=pl.DeviceIdType.MESH)
    pl.semaphore_wait(barrier, 8)

    def copy(n):
        src, dst, peer = plan[n]()
        return pltpu.make_async_remote_copy(
            src_ref=src,
            dst_ref=dst,
            send_sem=ss.at[n],
            recv_sem=rs.at[n],
            device_id=peer,
            device_id_type=pl.DeviceIdType.MESH,
        )

    def start(*numbers):
        for n in numbers:
            copy(n).start()

    def got(*numbers):
        for n in numbers:
            copy(n).wait_recv()

    def row_of(z_part, x_part, which):
        return g_pad.at[1 + 2 * (z_part * 4 + x_part) + which]

    def same(ref, peer):
        return ref, ref, peer

    def pair(block):
        return kall.at[block, c]

    def pairs(y_part):
        return kall.at[pl.ds(2 * y_part, 2), c]

    def part_of(s):
        return (y + 2 + 3 * s) % 4

    def half(ref, which):
        return ref.at[:, which * 40 : which * 40 + 40]

    def first_hop(k, which):
        block = 1 - zl if k == 0 else zl
        source = half(r1.at[2 * y_far + block, 0:2], which)
        return source, (ya, yb)[which].at[k], (to_yr, to_yl)[which]

    def second_hop(k, way, which):
        block = 1 - zl if k == 0 else zl
        y_part = (y_right, y_left)[way]
        return (
            half(r1.at[2 * y_part + block, 0:2], which),
            half((yl, yr)[way].at[k], which),
            (to_yr, to_yl)[way],
        )

    def rows_half(which):
        return pl.ds(which * 40, 40)

    def z_first(s):
        return r1.at[2 * part_of(s) + 1 - zl, 2], zb.at[part_of(s)], to_zl

    def tap_first(which):
        source = r1.at[2 * y_far + zl, 2, rows_half(which)]
        return source, (ba, bb)[which], (to_yr, to_yl)[which]

    def tap_second(way, which):
        y_part = (y_right, y_left)[way]
        source = r1.at[2 * y_part + zl, 2, rows_half(which)]
        return source, (bl, br)[way].at[rows_half(which)], (to_yr, to_yl)[way]

    plan = {
        0: lambda: (g_ref.at[0], row_of(zh, x, 0), to_z),
        1: lambda: (g_ref.at[1], row_of(zh, x, 1), to_z),
        2: lambda: (k_ref, kall.at[e, c, 1], to_z),
        3: lambda: (k_ref, kall.at[e, c, 0], to_zl),
        4: lambda: (k_ref, kall.at[e, c, 1], to_zx),
        5: lambda: (x_hbm.at[pl.ds(7 * oz, 9)], xz, to_z),
        6: lambda: (g_ref.at[0], row_of(zh, x, 0), to_xr),
        7: lambda: (g_ref.at[1], row_of(zh, x, 1), to_xr),
        8: lambda: (g_ref.at[1], row_of(zh, x, 1), to_xl),
        9: lambda: (g_ref.at[0], row_of(zh, x, 0), to_xl),
        10: lambda: same(row_of(zh, x_left, 0), to_xr),
        11: lambda: same(row_of(zh, x_right, 1), to_xl),
        12: lambda: same(row_of(oz, x, 0), to_xr),
        13: lambda: same(row_of(oz, x, 1), to_xr),
        14: lambda: same(row_of(oz, x, 0), to_xl),
        15: lambda: same(row_of(oz, x, 1), to_xl),
        16: lambda: same(row_of(oz, x_left, 1).at[0:64], to_xr),
        17: lambda: same(row_of(oz, x_right, 1).at[64:128], to_xl),
        18: lambda: (k_ref, kall.at[e, c, 0], to_yr),
        19: lambda: (k_ref, kall.at[e, c, 0], to_yl),
        20: lambda: same(kall.at[e, c, 1], to_yr),
        21: lambda: same(kall.at[e, c, 1], to_yl),
        22: lambda: same(pair(e_other), to_yr),
        23: lambda: same(pair(e_other), to_yl),
        24: lambda: same(pair(y_left * 2 + zl), to_yr),
        25: lambda: same(pair(y_right * 2 + 1 - zl), to_yl),
        26: lambda: same(pairs(y), to_core),
        27: lambda: same(pairs(y_left), to_core),
        28: lambda: same(pairs(y_right), to_core),
        29: lambda: same(pairs(y_far), to_core),
        30: lambda: (f.at[x_far, 0, near_half], xa.at[near_half], to_xr),
        31: lambda: (f.at[x_far, 1, near_half], xb.at[near_half], to_xl),
        32: lambda: (f.at[x_right, 1], xl.at[1], to_xr),
        33: lambda: (f.at[x_left, 0], xr.at[0], to_xl),
        34: lambda: (f.at[x_right, 0], xl.at[0], to_xr),
        35: lambda: (f.at[x_left, 1], xr.at[1], to_xl),
        36: lambda: first_hop(0, 0),
        37: lambda: first_hop(0, 1),
        38: lambda: first_hop(1, 0),
        39: lambda: first_hop(1, 1),
        40: lambda: second_hop(0, 0, 1),
        41: lambda: second_hop(0, 1, 0),
        42: lambda: second_hop(0, 0, 0),
        43: lambda: second_hop(0, 1, 1),
        44: lambda: second_hop(1, 0, 1),
        45: lambda: second_hop(1, 1, 0),
        46: lambda: second_hop(1, 0, 0),
        47: lambda: second_hop(1, 1, 1),
        48: lambda: (r1.at[2 * y + 1 - zl, 0:2], zr, to_zl),
        49: lambda: same(row_of(zh, x_far, 0), to_z),
        50: lambda: (f.at[x_far, 0, 1 - near_half], xa.at[1 - near_half], to_xr),
        51: lambda: (f.at[x_far, 1, 1 - near_half], xb.at[1 - near_half], to_xl),
        52: lambda: z_first(0),
        53: lambda: z_first(1),
        54: lambda: z_first(2),
        55: lambda: z_first(3),
        56: lambda: tap_first(0),
        57: lambda: tap_first(1),
        58: lambda: tap_second(0, 1),
        59: lambda: tap_second(1, 0),
        60: lambda: tap_second(0, 0),
        61: lambda: tap_second(1, 1),
    }

    def siblings(s):
        return pltpu.make_async_remote_copy(
            src_ref=p.at[pl.ds(2 * part_of(s), 2), 1 - c],
            dst_ref=r1.at[pl.ds(2 * part_of(s), 2)],
            send_sem=sc.at[0, s],
            recv_sem=sc.at[1, s],
            device_id=to_core,
            device_id_type=pl.DeviceIdType.MESH,
        )

    own_g = pltpu.make_async_copy(g_ref, g_pad.at[pl.ds(1 + 2 * t, 2)], lc.at[0])
    own_x = pltpu.make_async_copy(x_hbm, x_ref, lc.at[1])
    start(2, 6, 8, 18, 19, 3, 4, 7, 9, 1, 0, 5)
    own_x.start()
    own_g.start()

    kall[e, c, 0] = k_ref[...]
    g_pad[0] = jnp.zeros((128, 1280), BF)
    g_pad[17] = jnp.zeros((128, 1280), BF)

    def turn(z_part, x_part):
        at = z_part * 4 + x_part
        block = g_pad[pl.ds(1 + 2 * at, 2)].reshape(256, 1280)
        gt[:, :, pl.ds(pl.multiple_of(at * 256, 256), 256)] = block.T.reshape(16, 80, 256)

    xv[:, 0:128] = jnp.zeros((512, 128), BF)
    xv[:, 17 * 128 : 18 * 128] = jnp.zeros((512, 128), BF)

    def own_row(k, _):
        at = pl.multiple_of((k + 1) * 128, 128)
        xv[:, pl.ds(at, 128)] = three_shifts(x_ref[k]).astype(BF)
        return 0

    own_x.wait()
    lax.fori_loop(0, 16, own_row, 0)

    got(6)
    start(10)
    got(8)
    start(11)

    xt[0, 9 * zh] = jnp.zeros((128, 512), BF)
    xt[1, 9 * zh] = jnp.zeros((128, 512), BF)

    def own_turned(k, _):
        xt[0, k + 1 - zh] = three_shifts(x_ref[7 * zh + k]).T.astype(BF)
        return 0

    lax.fori_loop(0, 9, own_turned, 0)

    got(2)
    start(20, 21)
    got(3, 4)
    start(22, 23, 26)
    own_g.wait()
    turn(zh, x)
    got(18, 20)
    start(24)
    got(1)
    start(13, 15)
    got(7, 9)
    turn(zh, x_left)
    turn(zh, x_right)
    got(10)
    start(49)
    got(0)
    start(12, 14)
    turn(oz, x)
    got(23)
    start(25)
    got(22)
    start(27)
    got(19, 21)
    start(28)
    got(13)
    start(16)
    got(15)
    start(17)
    got(5)

    def other_turned(k, _):
        xt[1, k + 1 - zh] = three_shifts(xz[k]).T.astype(BF)
        return 0

    lax.fori_loop(0, 9, other_turned, 0)

    got(11)
    turn(zh, x_far)

    def forward_half(xq, h):
        left = jnp.concatenate(
            [xt[j, pl.ds(2 * xq + u, 2)].reshape(256, 512) for j in range(2) for u in range(3)],
            axis=1,
        )
        right = jnp.concatenate(
            [
                kall[pl.ds(4 * h, 4), :, j, u].reshape(640, 512)
                for j in range(2)
                for u in range(3)
            ],
            axis=1,
        )
        f[xq, :, h] = dot_nt(left, right).reshape(2, 128, 640)

    def forward(xq):
        left = jnp.concatenate(
            [xt[j, pl.ds(2 * xq + u, 2)].reshape(256, 512) for j in range(2) for u in range(3)],
            axis=1,
        )
        right = jnp.concatenate(
            [kall[:, :, j, u].reshape(1280, 512) for j in range(2) for u in range(3)], axis=1
        )
        sums = dot_nt(left, right).reshape(2, 128, 1280)
        for h in range(2):
            f[xq, :, h] = sums[:, :, h * 640 : h * 640 + 640]

    def kernel_terms(s, _):
        yq = part_of(s)
        left = gt[pl.ds(4 * yq, 4)].reshape(320, 2048)
        for u in range(3):
            part = dot_nt(left, xv[:, u * 128 : u * 128 + 2048])
            p[pl.ds(2 * yq, 2), :, u] = part.reshape(2, 2, 80, 512)
        siblings(s).start()
        return 0

    def joined(s):
        siblings(s).wait_recv()
        for k in range(2):
            at = 2 * part_of(s) + k
            r1[at] = r1[at] + p[at, c]

    def add_half(k, way):
        block = 1 - zl if k == 0 else zl
        at = 2 * (y_right, y_left)[way] + block
        rows = slice(way * 40, way * 40 + 40)
        r1[at, 0:2, rows] = r1[at, 0:2, rows] + (ya, yb)[way][k]

    def add_tap(s):
        at = 2 * part_of(s) + zl
        r1[at, 2] = r1[at, 2] + zb[part_of(s)]

    got(26, 27, 28)

    def first_chunk(s, _):
        h = (near_half + s) % 2
        forward_half(x_far, h)

        @pl.when(s == 0)
        def _():
            start(30, 31)
            got(24, 25)
            start(29)
            got(12, 14)
            turn(oz, x_left)
            turn(oz, x_right)
            got(29)

        return 0

    lax.fori_loop(0, 2, first_chunk, 0)
    start(50, 51)
    got(16, 17, 49)
    turn(oz, x_far)
    lax.fori_loop(0, 2, kernel_terms, 0)
    joined(0)
    start(36, 37, 38, 39, 52)

    def near(s, _):
        forward((x + 1 + 2 * s) % 4)

        @pl.when(s == 0)
        def _():
            start(32)

        return 0

    lax.fori_loop(0, 2, near, 0)
    start(33)
    got(30, 50)
    f[x_right, 0] = f[x_right, 0] + xa[...]
    start(34)
    got(31, 51)
    f[x_left, 1] = f[x_left, 1] + xb[...]
    start(35)

    def last_terms(s, _):
        kernel_terms(5 - s, 0)

        @pl.when(s == 2)
        def _():
            joined(1)
            start(40, 53)

        return 0

    lax.fori_loop(2, 4, last_terms, 0)
    joined(3)
    start(41, 55)
    got(36)
    add_half(0, 0)
    start(42)
    got(37)
    add_half(0, 1)
    start(43, 44, 45)
    got(38)
    add_half(1, 0)
    start(46)
    got(39)
    add_half(1, 1)
    start(47)
    joined(2)
    start(54)
    got(52)
    add_tap(0)
    start(56, 57)
    got(53)
    add_tap(1)
    start(58)
    got(55)
    add_tap(3)
    start(59)
    forward(x)

    lane = lax.broadcasted_iota(jnp.int32, (160, 128), 1)

    def put_in(s):
        rows = pl.ds(4 * s, 4)
        return pltpu.make_async_copy(in_ref.at[rows], in_hbm.at[rows], lc.at[2 + s])

    def put_conv(k):
        return pltpu.make_async_copy(conv_ref.at[k], conv_hbm.at[k], lc.at[6 + k])

    def input_grad(s, _):
        left = jnp.concatenate(
            [g_pad[pl.ds(4 * s + 2 - u, 4)].reshape(512, 1280) for u in range(3)], axis=1
        )
        right = jnp.concatenate([kall[:, :, 0, u].reshape(1280, 512) for u in range(3)], axis=0)
        turned = jnp.dot(left, right, preferred_element_type=F32).T
        for k in range(4):
            at = slice(k * 128, (k + 1) * 128)
            first = jnp.where(lane == 127, 0.0, pltpu.roll(turned[0:160, at], 127, 1))
            last = jnp.where(lane == 0, 0.0, pltpu.roll(turned[320:480, at], 1, 1))
            in_ref[4 * s + k] = (first + turned[160:320, at] + last).astype(BF)
        put_in(s).start()

        @pl.when(s == 1)
        def _():
            got(40, 41, 42, 43)
            at = 2 * y + 1 - zl
            r1[at, 0:2] = r1[at, 0:2] + yl[0] + yr[0]
            start(48)

        @pl.when(s == 2)
        def _():
            got(56)
            rows = slice(0, 40)
            r1[2 * y_right + zl, 2, rows] = r1[2 * y_right + zl, 2, rows] + ba[...]
            start(60)
            got(57)
            rows = slice(40, 80)
            r1[2 * y_left + zl, 2, rows] = r1[2 * y_left + zl, 2, rows] + bb[...]
            start(61)

        return 0

    lax.fori_loop(0, 4, input_grad, 0)

    def spread(u, terms):
        for q in range(4):
            lin[q] = terms[:, q * 128 : q * 128 + 128]
        fours = [
            jnp.concatenate([lin[q, pl.ds(j, 20, stride=4), :] for q in range(4)], axis=1)
            for j in range(4)
        ]
        for v in range(3):
            a = [four[:, v * 160 : v * 160 + 160] for four in fours]
            fives = [
                a[0][:, :128],
                jnp.concatenate([a[0][:, 128:], a[1][:, :96]], axis=1),
                jnp.concatenate([a[1][:, 96:], a[2][:, :64]], axis=1),
                jnp.concatenate([a[2][:, 64:], a[3][:, :32]], axis=1),
                a[3][:, 32:],
            ]
            for m in range(5):
                kgrad_ref[pl.ds((3 * u + v) * 100 + m, 20, stride=5), :] = fives[m]

    got(54)
    add_tap(2)
    got(44, 45, 46, 47, 48)
    spread(0, r1[2 * y + zl, 0] + yl[1, 0] + yr[1, 0] + zr[0])
    spread(1, r1[2 * y + zl, 1] + yl[1, 1] + yr[1, 1] + zr[1])
    got(58, 59, 60, 61)
    spread(2, r1[2 * y + zl, 2] + bl[...] + br[...])
    for k, numbers in ((1, (32, 35)), (0, (33, 34))):
        got(*numbers)
        for h in range(2):
            total = f[x, k, h] + xl[k, h] + xr[k, h]
            conv_ref[k, :, h * 640 : h * 640 + 640] = total.astype(BF)
        put_conv(k).start()

    for s in range(4):
        put_in(s).wait()
    for k in range(2):
        put_conv(k).wait()
    for n in plan:
        copy(n).wait_send()
    for s in range(4):
        siblings(s).wait_send()


def on_device(latents, kernel, out_grad):
    g = out_grad.reshape(2, 128, 1280)
    xs = latents.reshape(16, 160, 128)
    k = kernel.reshape(3, 3, 80, 160).transpose(0, 2, 1, 3).reshape(3, 80, 480)
    k = jnp.pad(k, ((0, 0), (0, 0), (0, 32)))
    vmem = pl.BlockSpec(memory_space=pltpu.VMEM)
    hbm = pl.BlockSpec(memory_space=pl.ANY)
    scratch = [
        ((16, 160, 128), BF),
        ((2, 128, 1280), BF),
        ((16, 160, 128), BF),
        ((18, 128, 1280), BF),
        ((16, 80, 2048), BF),
        ((8, 2, 2, 3, 80, 512), BF),
        ((9, 160, 128), BF),
        ((512, 2304), BF),
        ((2, 10, 128, 512), BF),
        ((4, 2, 2, 128, 640), F32),
        ((2, 128, 640), F32),
        ((2, 128, 640), F32),
        ((2, 2, 128, 640), F32),
        ((2, 2, 128, 640), F32),
        ((8, 2, 3, 80, 512), F32),
        ((8, 3, 80, 512), F32),
        ((2, 2, 40, 512), F32),
        ((2, 2, 40, 512), F32),
        ((2, 2, 80, 512), F32),
        ((2, 2, 80, 512), F32),
        ((2, 80, 512), F32),
        ((4, 80, 512), F32),
        ((40, 512), F32),
        ((40, 512), F32),
        ((80, 512), F32),
        ((80, 512), F32),
        ((4, 80, 128), F32),
    ]
    conv, grad, kgrad = pl.pallas_call(
        body,
        out_shape=(
            jax.ShapeDtypeStruct((2, 128, 1280), BF),
            jax.ShapeDtypeStruct((16, 160, 128), BF),
            jax.ShapeDtypeStruct((900, 128), F32),
        ),
        in_specs=[hbm, hbm, vmem],
        out_specs=(hbm, hbm, vmem),
        scratch_shapes=[pltpu.VMEM(shape, dtype) for shape, dtype in scratch]
        + [pltpu.SemaphoreType.DMA(shape) for shape in ((N_COPIES,), (N_COPIES,), (2, 4), (8,))],
        compiler_params=pltpu.CompilerParams(
            collective_id=0, has_side_effects=True, vmem_limit_bytes=67043328
        ),
        name="conv_all",
    )(g, xs, k)
    return (
        conv.reshape(2, 1, 128, 1280),
        grad.reshape(16, 1, 160, 128),
        kgrad.reshape(9, 1, 1, 12800),
    )


def solution(mesh):
    return jax.shard_map(
        on_device,
        mesh=mesh,
        in_specs=(
            P(None, "dp", "tensor", None),
            P(None, "dp", "tensor", None),
            P("tensor", "dp", None, None),
        ),
        out_specs=(
            P("tensor", "dp", None, None),
            P(None, "dp", "tensor", None),
            P(None, "dp", "tensor", None),
        ),
        check_vma=False,
    )
```
